128 devices in a mesh: chan: 16 (over z, y), seg: 4 (over x_hi, core), lag: 2 (over x_lo).
Axes of the slice: x: 4 (x_hi: 2, x_lo: 2; x = x_hi * 2 + x_lo), y: 4, z: 4, core: 2. Of those that a mesh axis runs over, the one named last changes fastest.
Arguments:
- spectra: bfloat16 [4, 10000, 2, 6144], P('seg', 'chan', None, 'lag'), may hold values from -6 to 6
- pair_local: int32 [16, 3, 256], replicated, may hold values from 0 to 624
- pair_partner: int32 [16, 3, 256], replicated, may hold values from 0 to 624, as said below
- pair_bin: int32 [16, 3, 256], replicated, may hold values from 0 to 1
- pair_owner: int32 [16, 3, 256], replicated, may hold values 0 or 1
- pair_count: int32 [16, 3], replicated, may hold values from 64 to 256, as said below
Outputs:
- stacks: float32 [10000, 2, 2048], P('chan', None, 'lag')
The draws below stay inside these ranges and needn't reach their ends.
Inputs may be any that keep to these rules, and one draw needn't show every extreme that they name: `pair_partner`: in round 0 the two channels of a pair differ. `pair_count`: some block reaches 256 in some round.
All inputs are finite; a program needn't handle non-finite values.
Results may differ from the reference program's by a relative error of at most 0.0065.
Values may be sent and summed in bfloat16 or wider, within the bound.
No kernel may reach another device: no remote copies, remote signals or barrier semaphores. Data moves between devices by JAX's collectives and lax.ppermute only.
A program may use at most 128 MiB of HBM per device.

```python
import math
import jax
import jax.numpy as jnp
from jax import lax

FREQ = 6144
LAGS = 2048
CB = 625
PAIRS = 256
ROUNDS = 3
BINS = 2
SEGS = 4
BLOCKS = 16
CHANNELS = 10000


def pair_fields(key):
    base_key = jax.random.fold_in(key, 7)
    local_ids = jax.random.randint(jax.random.fold_in(base_key, 1), (BLOCKS, ROUNDS, PAIRS), 0, CB)
    step_ids = jax.random.randint(jax.random.fold_in(base_key, 2), (BLOCKS, ROUNDS, PAIRS), 1, CB)
    return (local_ids.astype(jnp.int32), jnp.mod(local_ids + step_ids, CB).astype(jnp.int32))


def draw_pair_local(key, part):
    return pair_fields(key)[0]


def draw_pair_partner(key, part):
    return pair_fields(key)[1]


def draw_pair_count(key, part):
    counts = jax.random.randint(jax.random.fold_in(key, 11), (BLOCKS * ROUNDS,), max(PAIRS // 4, 1), PAIRS + 1)
    chosen = jax.random.randint(jax.random.fold_in(key, 13), (), 0, BLOCKS * ROUNDS)
    counts = jnp.where(jnp.arange(BLOCKS * ROUNDS, dtype=jnp.int32) == chosen, PAIRS, counts)
    return counts.reshape(BLOCKS, ROUNDS).astype(jnp.int32)


def plant(entries, key, low, high):
    shape = entries.shape
    place = [jax.random.randint(jax.random.fold_in(key, axis), (), 0, shape[axis]) for axis in range(len(shape))]
    entries = entries.at[tuple(place)].set(low)
    longest = shape.index(max(shape))
    place[longest] = (place[longest] + 1) % shape[longest]
    return entries.at[tuple(place)].set(high)


def block_scale(rng, extent, pieces, low, largest):
    level = 1.0
    for axis_at, blocks in pieces:
        heights = jax.random.uniform(jax.random.fold_in(jax.random.fold_in(rng, 6), axis_at), (blocks,), jnp.float32, low / len(pieces), largest / len(pieces))
        level = level * jnp.repeat(jnp.exp(heights), extent[axis_at] // blocks).reshape((-1,) + (1,) * (len(extent) - 1 - axis_at))
    return level


def gaussian(own_key, dims, spread, bound, pieces=(), held_as=jnp.bfloat16):
    result = spread * jax.random.normal(own_key, dims, jnp.float32)
    if pieces:
        result = result * block_scale(own_key, dims, pieces, -0.22, 0.18)
    return jnp.clip(result, -bound, bound).astype(held_as)


def setup_inputs(seed: int = 0) -> dict:
    keys = jax.random.split(jax.random.key(seed), 7)
    return {
        "spectra": gaussian(keys[0], (SEGS, CHANNELS, 2, FREQ), 0.7, 6.0, ((0, 4), (1, 16), (3, 2))),
        "pair_local": draw_pair_local(jax.random.fold_in(keys[6], 71), 0),
        "pair_partner": draw_pair_partner(jax.random.fold_in(keys[6], 71), 0),
        "pair_bin": plant(jax.random.randint(keys[3], (BLOCKS, ROUNDS, PAIRS), 0, BINS), jax.random.fold_in(keys[3], 1), 0, BINS - 1).astype(jnp.int32),
        "pair_owner": plant((jax.random.randint(keys[4], (BLOCKS, ROUNDS, PAIRS), 0, 2) < 1).astype(jnp.int32), jax.random.fold_in(keys[4], 1), 0, 1),
        "pair_count": draw_pair_count(jax.random.fold_in(keys[6], 71), 0),
    }


def table_rows(taus):
    freq_index = jnp.arange(FREQ, dtype=jnp.int32) + 1
    phase = jnp.mod(taus[:, None] * freq_index[None, :], 2 * FREQ)
    angle = phase.astype(jnp.float32) * (math.pi / FREQ)
    return jnp.concatenate([jnp.cos(angle), -jnp.sin(angle)], axis=1).astype(jnp.bfloat16)


def reference(spectra, pair_local, pair_partner, pair_bin, pair_owner, pair_count):
    taus = jnp.arange(LAGS, dtype=jnp.int32) - LAGS // 2
    table = table_rows(taus).astype(jnp.float32)
    corr_scale = FREQ ** -0.5
    blocks = spectra.reshape(SEGS, BLOCKS, CB, 2, FREQ)
    stacks = jnp.zeros((CHANNELS * BINS, LAGS), jnp.float32)
    for round_index in range(ROUNDS):
        def one_block(block_index):
            partner_index = jnp.mod(block_index + round_index, BLOCKS)
            first = jnp.take(blocks, block_index, axis=1)
            second = jnp.take(blocks, partner_index, axis=1)
            first = jnp.take(first, pair_local[block_index, round_index], axis=1).astype(jnp.float32)
            second = jnp.take(second, pair_partner[block_index, round_index], axis=1).astype(jnp.float32)
            cross_real = first[:, :, 0] * second[:, :, 0] + first[:, :, 1] * second[:, :, 1]
            cross_imag = first[:, :, 1] * second[:, :, 0] - first[:, :, 0] * second[:, :, 1]
            cross = jnp.concatenate([cross_real, cross_imag], axis=2).astype(jnp.bfloat16).astype(jnp.float32)
            corr = jnp.einsum("spf,tf->spt", cross, table) * corr_scale
            return jnp.sum(corr, axis=0)
        corr_all = lax.map(one_block, jnp.arange(BLOCKS, dtype=jnp.int32))
        block_ids = jnp.arange(BLOCKS, dtype=jnp.int32)[:, None]
        partner_ids = jnp.mod(block_ids + round_index, BLOCKS)
        first_chan = block_ids * CB + pair_local[:, round_index]
        second_chan = partner_ids * CB + pair_partner[:, round_index]
        target = jnp.where(pair_owner[:, round_index] == 0, first_chan, second_chan)
        target_rows = (target * BINS + pair_bin[:, round_index]).reshape(-1)
        live = (jnp.arange(PAIRS, dtype=jnp.int32)[None, :] < pair_count[:, round_index][:, None]).astype(jnp.float32)
        weighted = (corr_all * live[:, :, None]).reshape(BLOCKS * PAIRS, LAGS)
        stacks = stacks.at[target_rows].add(weighted)
    return stacks.reshape(CHANNELS, BINS, LAGS)
```

```python
import math

import jax
import jax.numpy as jnp
from jax import lax
from jax.sharding import PartitionSpec as P

FREQ = 6144
LAGS = 2048
BINS = 2
HALF = 128


def route(axis, move):
    return [(i, move(i)) for i in range(lax.axis_size(axis))]


def shifted(value, distance):
    count = lax.axis_size("chan")
    return lax.ppermute(value, "chan", route("chan", lambda i: (i + distance) % count))


def swapped(value, axis, bit):
    return lax.ppermute(value, axis, route(axis, lambda i: i ^ bit))


def lag_table(freq_index, lag_start):
    fine = 32
    coarse = LAGS // fine

    def waves(taus):
        phase = jnp.mod(taus[:, None] * freq_index[None, :], 2 * FREQ)
        angle = phase.astype(jnp.float32) * (math.pi / FREQ)
        return jnp.cos(angle), jnp.sin(angle)

    cos_a, sin_a = waves(lag_start)
    cos_b, sin_b = waves(jnp.arange(fine, dtype=jnp.int32))
    cos_a, sin_a, cos_b, sin_b = lax.optimization_barrier((cos_a, sin_a, cos_b, sin_b))
    cos_a, sin_a = cos_a[:, None, :], sin_a[:, None, :]
    cos_b, sin_b = cos_b[None, :, :], sin_b[None, :, :]
    cos_ab = (cos_a * cos_b - sin_a * sin_b).astype(jnp.bfloat16)
    minus_sin_ab = (-(sin_a * cos_b + cos_a * sin_b)).astype(jnp.bfloat16)
    table = jnp.concatenate([cos_ab, minus_sin_ab], axis=2)
    return table.reshape(coarse * fine, 2 * freq_index.shape[0])


def per_device(spectra, pair_local, pair_partner, pair_bin, pair_owner, pair_count):
    block = lax.axis_index("chan")
    blocks = lax.axis_size("chan")
    lag_index = lax.axis_index("lag")
    core = lax.axis_index("seg") % 2
    own = spectra[0]
    chans, _, half_freq = own.shape
    rows = own.reshape(chans, 2 * half_freq)
    before, before2, after = (block - 1) % blocks, (block - 2) % blocks, (block + 1) % blocks
    scale = FREQ ** (-0.5)

    chan_ids = jnp.arange(chans, dtype=jnp.int32)

    def pick(index):
        one_hot = (index[:, None] == chan_ids[None, :]).astype(jnp.bfloat16)
        return lax.dot_general(
            one_hot, rows, (((1,), (0,)), ((), ())), preferred_element_type=jnp.float32
        ).astype(jnp.bfloat16)

    up = [
        pair_local[block, 1, HALF:],
        pair_local[block, 2, :HALF],
        pair_local[block, 2, HALF:],
    ]
    down = [
        pair_partner[before, 1, :HALF],
        pair_partner[before2, 2, :HALF],
        pair_partner[before2, 2, HALF:],
    ]
    from_before = [shifted(pick(index), 1) for index in up]
    from_after = [shifted(pick(index), -1) for index in down]

    quarter = LAGS // 4
    flips = jnp.arange(LAGS // 32, dtype=jnp.int32)
    lag_flip, core_flip, step = flips // 32, (flips // 16) % 2, flips % 16
    lag_start = (
        (lag_index ^ lag_flip) * (2 * quarter) + (core ^ core_flip) * quarter + step * 32
    ) - LAGS // 2
    freq_index = lag_index * half_freq + jnp.arange(half_freq, dtype=jnp.int32) + 1
    table = lag_table(freq_index, lag_start)

    def correlate(first, second):
        first = first.astype(jnp.float32)
        second = second.astype(jnp.float32)
        first_re, first_im = first[:, :half_freq], first[:, half_freq:]
        second_re, second_im = second[:, :half_freq], second[:, half_freq:]
        cross = jnp.concatenate(
            [
                first_re * second_re + first_im * second_im,
                first_im * second_re - first_re * second_im,
            ],
            axis=1,
        ).astype(jnp.bfloat16)
        part = (
            lax.dot_general(
                cross, table, (((1,), (1,)), ((), ())), preferred_element_type=jnp.float32
            )
            * scale
        )
        keep0, send0 = part[:, :quarter], part[:, quarter : 2 * quarter]
        keep1, send1 = part[:, 2 * quarter : 3 * quarter], part[:, 3 * quarter :]
        other = swapped(jnp.concatenate([send0, send1], axis=1).astype(jnp.bfloat16), "seg", 1)
        keep0 = keep0 + other[:, :quarter].astype(jnp.float32)
        keep1 = keep1 + other[:, quarter:].astype(jnp.float32)
        other = swapped(keep1.astype(jnp.bfloat16), "lag", 1)
        mine = (keep0 + other.astype(jnp.float32)).astype(jnp.bfloat16)
        other = swapped(mine, "seg", 2)
        return (mine.astype(jnp.float32) + other.astype(jnp.float32)).astype(jnp.bfloat16)

    both = pick(jnp.concatenate([pair_local[block, 0], pair_partner[block, 0]]))
    slots = pair_local.shape[2]
    corr0 = correlate(both[:slots], both[slots:])
    near = pick(jnp.concatenate([pair_local[block, 1, :HALF], pair_partner[before, 1, HALF:]]))
    corr1 = correlate(
        jnp.concatenate([near[:HALF], from_before[0]]),
        jnp.concatenate([from_after[0], near[HALF:]]),
    )
    corr2a = correlate(from_before[1], from_after[1])
    corr2b = correlate(from_before[2], from_after[2])

    to_after = [corr1[:HALF], corr2a, corr2b]
    to_before = [corr1[HALF:], corr2a, corr2b]
    parts = [corr0, corr1[:HALF], corr1[HALF:]]
    parts += [shifted(value, 1) for value in to_after]
    parts += [shifted(value, -1) for value in to_before]

    slot_ids = jnp.arange(slots, dtype=jnp.int32)

    def targets(source, round_index, chosen, owner):
        index = pair_local if owner == 0 else pair_partner
        live = slot_ids < pair_count[source, round_index]
        hit = live & (pair_owner[source, round_index] == owner)
        row = index[source, round_index] * BINS + pair_bin[source, round_index]
        return jnp.where(hit, row, -1)[chosen]

    every, low, high = slice(None), slice(0, HALF), slice(HALF, None)
    live0 = slot_ids < pair_count[block, 0]
    chan0 = jnp.where(pair_owner[block, 0] == 0, pair_local[block, 0], pair_partner[block, 0])
    row_ids = jnp.concatenate(
        [
            jnp.where(live0, chan0 * BINS + pair_bin[block, 0], -1),
            targets(block, 1, low, 0),
            targets(before, 1, high, 1),
            targets(before, 1, low, 1),
            targets(before2, 2, every, 1),
            targets(block, 1, high, 0),
            targets(block, 2, every, 0),
        ]
    )
    mine = jnp.concatenate(parts, axis=0)
    other = swapped(mine, "seg", 1)
    low_core = core == 0
    corr = jnp.concatenate(
        [jnp.where(low_core, mine, other), jnp.where(low_core, other, mine)], axis=1
    )
    stack_ids = jnp.arange(chans * BINS, dtype=jnp.int32)
    selector = (stack_ids[:, None] == row_ids[None, :]).astype(jnp.bfloat16)
    stacks = lax.dot_general(
        selector, corr, (((1,), (0,)), ((), ())), preferred_element_type=jnp.float32
    )
    return stacks.reshape(chans, BINS, LAGS // 2)


def solution(mesh):
    return jax.shard_map(
        per_device,
        mesh=mesh,
        in_specs=(P("seg", "chan", None, "lag"), P(), P(), P(), P(), P()),
        out_specs=P("chan", None, "lag"),
        check_vma=False,
    )
```

```python
import functools
import math

import jax
import jax.numpy as jnp
from jax import lax
from jax.experimental import pallas as pl
from jax.experimental.pallas import tpu as pltpu
from jax.sharding import PartitionSpec as P

FREQ = 6144
LAGS = 2048
BINS = 2
HALF = 128
QUARTER = LAGS // 4
TILE = 512
PICK_MB = 20
CORR_MB = 56
F32 = jnp.float32
BF16 = jnp.bfloat16


def route(axis, move):
    return [(i, move(i)) for i in range(lax.axis_size(axis))]


def shifted(value, distance):
    count = lax.axis_size("chan")
    return lax.ppermute(value, "chan", route("chan", lambda i: (i + distance) % count))


def swapped(value, axis, bit):
    return lax.ppermute(value, axis, route(axis, lambda i: i ^ bit))


def params(megabytes=32):
    return pltpu.CompilerParams(vmem_limit_bytes=megabytes << 20)


def dot(a, b):
    return jnp.dot(a, b, preferred_element_type=F32)


def cost(flops, moved):
    return pl.CostEstimate(flops=flops, bytes_accessed=moved, transcendentals=0)


def pick_kernel(index_ref, rows_ref, *refs):
    outs, hot_ref = refs[:-1], refs[-1]

    @pl.when(pl.program_id(0) == 0)
    def _():
        ids = lax.broadcasted_iota(jnp.int32, hot_ref.shape, 1)
        hot_ref[...] = jnp.where(index_ref[...] == ids, 1.0, 0.0).astype(BF16)

    for part in range(2):
        picked = dot(hot_ref[...], rows_ref[part]).astype(BF16)
        row = 0
        for out_ref in outs:
            count = out_ref.shape[1]
            out_ref[part] = picked[row : row + count]
            row += count


def pick(groups, rows):
    counts = [sum(index.shape[0] for index in group) for group in groups]
    index = jnp.concatenate([index for group in groups for index in group])
    (total,), (_, chans, freqs) = index.shape, rows.shape
    return pl.pallas_call(
        pick_kernel,
        out_shape=[jax.ShapeDtypeStruct((2, count, freqs), BF16) for count in counts],
        grid=(freqs // TILE,),
        in_specs=[
            pl.BlockSpec((total, 1), lambda i: (0, 0)),
            pl.BlockSpec((2, chans, TILE), lambda i: (0, 0, i)),
        ],
        out_specs=[pl.BlockSpec((2, count, TILE), lambda i: (0, 0, i)) for count in counts],
        scratch_shapes=[pltpu.VMEM((total, chans), BF16)],
        compiler_params=params(PICK_MB),
        cost_estimate=cost(4 * total * chans * freqs, 4 * (chans + total) * freqs),
        name="pick",
    )(index[:, None], rows)


def table_kernel(coarse_ref, fine_ref, sign_ref, out_ref):
    cos_b, sin_b = fine_ref[0], fine_ref[1]
    width = cos_b.shape[1]
    for step in range(2 * QUARTER // width):
        cos_a, sin_a = coarse_ref[0, :, step : step + 1], coarse_ref[1, :, step : step + 1]
        cols = slice(step * width, (step + 1) * width)
        out_ref[0, :, cols] = (cos_a * cos_b - sin_a * sin_b).astype(BF16)
        out_ref[1, :, cols] = (sign_ref[0] * (sin_a * cos_b + cos_a * sin_b)).astype(BF16)


def lag_table(freq_index, core, sign):
    freqs, width = freq_index.shape[0], 128
    steps = 2 * QUARTER // width
    step = jnp.arange(steps, dtype=jnp.int32)
    start = (core ^ (step // (steps // 2))) * QUARTER + (step % (steps // 2)) * width

    def waves(doubled, freq):
        angle = jnp.mod(doubled * freq, 4 * FREQ).astype(F32) * (math.pi / (2 * FREQ))
        return jnp.stack([jnp.cos(angle), jnp.sin(angle)])

    coarse = waves(2 * start[:, None], freq_index[None, :]).transpose(0, 2, 1)
    odd = 2 * jnp.arange(width, dtype=jnp.int32) + 1
    fine = waves(odd[None, :], freq_index[:, None])
    return pl.pallas_call(
        table_kernel,
        out_shape=jax.ShapeDtypeStruct((2, freqs, 2 * QUARTER), BF16),
        grid=(freqs // TILE,),
        in_specs=[
            pl.BlockSpec((2, TILE, steps), lambda i: (0, i, 0)),
            pl.BlockSpec((2, TILE, width), lambda i: (0, i, 0)),
            pl.BlockSpec(memory_space=pltpu.SMEM),
        ],
        out_specs=pl.BlockSpec((2, TILE, 2 * QUARTER), lambda i: (0, i, 0)),
        compiler_params=params(),
        cost_estimate=cost(12 * freqs * LAGS, 4 * freqs * LAGS),
        name="table",
    )(coarse, fine, sign[None])


def corr_kernel(count, *refs):
    firsts, seconds = refs[:count], refs[count : 2 * count]
    turn_ref, table_ref, keep_ref, send_ref, cos_acc, sin_acc = refs[2 * count :]
    step = pl.program_id(0)

    @pl.when(step == 0)
    def _():
        cos_acc[...] = jnp.zeros_like(cos_acc)
        sin_acc[...] = jnp.zeros_like(sin_acc)

    turn_cos, turn_sin = turn_ref[0:1], turn_ref[1:2]
    row = 0
    for first_ref, second_ref in zip(firsts, seconds):
        first_re, first_im = first_ref[0].astype(F32), first_ref[1].astype(F32)
        second_re, second_im = second_ref[0].astype(F32), second_ref[1].astype(F32)
        real = first_re * second_re + first_im * second_im
        imag = first_im * second_re - first_re * second_im
        turned_re = (real * turn_cos + imag * turn_sin).astype(BF16)
        turned_im = (imag * turn_cos - real * turn_sin).astype(BF16)
        here = slice(row, row + first_ref.shape[1])
        cos_acc[here] += dot(turned_re, table_ref[0])
        sin_acc[here] += dot(turned_im, table_ref[1])
        row += first_ref.shape[1]

    @pl.when(step == pl.num_programs(0) - 1)
    def _():
        scale = FREQ ** (-0.5)
        total = (cos_acc[...] + sin_acc[...]) * scale
        other = (cos_acc[...] - sin_acc[...]) * scale
        keep_ref[0] = total[:, :QUARTER]
        keep_ref[1] = other[:, :QUARTER]
        send_ref[0] = total[:, QUARTER:].astype(BF16)
        send_ref[1] = other[:, QUARTER:].astype(BF16)


def correlate(pairs, turn, table):
    firsts, seconds = zip(*pairs)
    rows = sum(count for _, count, _ in firsts)
    freqs = table.shape[1]

    def spec(value):
        _, count, place = value
        return pl.BlockSpec((2, count, TILE), lambda i: (0, place, i))

    flat = firsts + seconds
    return pl.pallas_call(
        functools.partial(corr_kernel, len(pairs)),
        out_shape=(
            jax.ShapeDtypeStruct((2, rows, QUARTER), F32),
            jax.ShapeDtypeStruct((2, rows, QUARTER), BF16),
        ),
        grid=(freqs // TILE,),
        in_specs=[spec(value) for value in flat]
        + [
            pl.BlockSpec((2, TILE), lambda i: (0, i)),
            pl.BlockSpec((2, TILE, 2 * QUARTER), lambda i: (0, i, 0)),
        ],
        out_specs=(
            pl.BlockSpec((2, rows, QUARTER), lambda i: (0, 0, 0)),
            pl.BlockSpec((2, rows, QUARTER), lambda i: (0, 0, 0)),
        ),
        scratch_shapes=[pltpu.VMEM((rows, 2 * QUARTER), F32)] * 2,
        compiler_params=params(CORR_MB),
        cost_estimate=cost(4 * rows * freqs * LAGS, 4 * freqs * LAGS + 16 * rows * freqs),
        name="corr",
    )(*[value[0] for value in flat], turn, table)


def fold_kernel(keep_ref, other_ref, mine_ref, far_ref):
    mine_ref[...] = (keep_ref[0] + other_ref[0].astype(F32)).astype(BF16)
    far_ref[...] = (keep_ref[1] + other_ref[1].astype(F32)).astype(BF16)


def fold(keep, other):
    shape = jax.ShapeDtypeStruct(keep.shape[1:], BF16)
    return pl.pallas_call(
        fold_kernel, out_shape=(shape, shape), compiler_params=params(), name="fold"
    )(keep, other)


def sum_kernel(flip_ref, mine_ref, near_ref, far_ref, across_ref, out_ref):
    total = (mine_ref[...].astype(F32) + near_ref[...].astype(F32)) + (
        far_ref[...].astype(F32) + across_ref[...].astype(F32)
    )
    total = total.astype(BF16)
    size = total.shape[1]
    row = lax.broadcasted_iota(jnp.int32, (size, size), 0)
    col = lax.broadcasted_iota(jnp.int32, (size, size), 1)
    wanted = jnp.where(flip_ref[0] == 1, size - 1 - col, col)
    order = jnp.where(row == wanted, 1.0, 0.0).astype(BF16)
    out_ref[...] = dot(total, order).astype(BF16)


def reduced(partial, flip):
    keep, send = partial
    mine, far = fold(keep, swapped(send, "seg", 1))
    near = swapped(far, "lag", 1)
    opposite = swapped(mine, "seg", 2)
    seg, lag = lax.axis_size("seg"), lax.axis_size("lag")
    pairs = [(s * lag + g, (s ^ 2) * lag + (g ^ 1)) for s in range(seg) for g in range(lag)]
    across = lax.ppermute(far, ("seg", "lag"), pairs)
    vmem = pl.BlockSpec(memory_space=pltpu.VMEM)
    return pl.pallas_call(
        sum_kernel,
        out_shape=jax.ShapeDtypeStruct(mine.shape, BF16),
        in_specs=[pl.BlockSpec(memory_space=pltpu.SMEM)] + [vmem] * 4,
        compiler_params=params(),
        name="sum4",
    )(flip[None], mine, near, opposite, across)


def final_kernel(at_ref, ids_ref, early_ref, early2_ref, late_ref, late2_ref, out_ref):
    chans = out_ref.shape[0]
    base = pl.program_id(0) * chans
    early = early_ref.shape[0]
    slots = ids_ref.shape[1]
    for bin_index in range(BINS):
        chan = base + lax.broadcasted_iota(jnp.int32, (chans, slots), 0)
        hot = jnp.where(ids_ref[...] == chan * BINS + bin_index, 1.0, 0.0).astype(BF16)
        mine = dot(hot[:, :early], early_ref[...]) + dot(hot[:, early:], late_ref[...])
        other = dot(hot[:, :early], early2_ref[...]) + dot(hot[:, early:], late2_ref[...])
        low = at_ref[0] == 0
        out_ref[:, bin_index, :QUARTER] = jnp.where(low, mine, other)
        out_ref[:, bin_index, QUARTER:] = jnp.where(low, other, mine)


def final(at, ids, early, early2, late, late2, chans):
    tile = 128
    whole = [pl.BlockSpec(v.shape, lambda i: (0, 0)) for v in (ids, early, early2, late, late2)]
    return pl.pallas_call(
        final_kernel,
        out_shape=jax.ShapeDtypeStruct((chans, BINS, LAGS // 2), F32),
        grid=(pl.cdiv(chans, tile),),
        in_specs=[pl.BlockSpec(memory_space=pltpu.SMEM)] + whole,
        out_specs=pl.BlockSpec((tile, BINS, LAGS // 2), lambda i: (i, 0, 0)),
        compiler_params=params(48),
        name="final",
    )(at[None], ids, early, early2, late, late2)


def per_device(spectra, pair_local, pair_partner, pair_bin, pair_owner, pair_count):
    block = lax.axis_index("chan")
    blocks = lax.axis_size("chan")
    lag_index = lax.axis_index("lag")
    core = lax.axis_index("seg") % 2
    own = spectra[0]
    chans, _, half_freq = own.shape
    slots = pair_local.shape[2]
    rows = own.transpose(1, 0, 2)
    before, before2 = (block - 1) % blocks, (block - 2) % blocks

    first_up = [pair_local[block, 1, HALF:], pair_local[block, 2, :HALF]]
    first_down = [pair_partner[before, 1, :HALF], pair_partner[before2, 2, :HALF]]
    last_up, last_down = pair_local[block, 2, HALF:], pair_partner[before2, 2, HALF:]
    picked = pick([first_up, first_down], rows)
    picked, rows, zero = lax.optimization_barrier((picked, rows, jnp.int32(0)))
    from_before, from_after = [shifted(picked[0], 1)], [shifted(picked[1], -1)]

    freq_index = lag_index * half_freq + jnp.arange(half_freq, dtype=jnp.int32) + 1 + zero
    sign = jnp.where(lag_index == 0, 1.0, -1.0).astype(F32)
    table = lag_table(freq_index, core, sign)
    angle = freq_index.astype(F32) * (math.pi / (2 * FREQ))
    turn = jnp.stack([jnp.cos(angle), jnp.sin(angle)])

    (local,) = pick(
        [
            [
                pair_local[block, 0] + zero,
                pair_partner[block, 0],
                pair_local[block, 1, :HALF],
                pair_partner[before, 1, HALF:],
            ]
        ],
        rows,
    )
    flip = 1 - lag_index

    def at(value, count, place):
        return value, count, place

    def total(pairs):
        return reduced(correlate(pairs, turn, table), flip)

    partial0 = correlate([(at(local, slots, 0), at(local, slots, 1))], turn, table)
    partial0, last_up, last_down = lax.optimization_barrier((partial0, last_up, last_down))
    picked = pick([[last_up], [last_down]], rows)
    from_before.append(shifted(picked[0], 1))
    from_after.append(shifted(picked[1], -1))
    corr0 = reduced(partial0, flip)
    corr1 = total(
        [
            (at(local, HALF, 4), at(from_after[0], HALF, 0)),
            (at(from_before[0], HALF, 0), at(local, HALF, 5)),
            (at(from_before[0], HALF, 1), at(from_after[0], HALF, 1)),
        ]
    )
    corr2 = total([(at(from_before[1], HALF, 0), at(from_after[1], HALF, 0))])
    to_after = jnp.concatenate([corr1[:HALF], corr1[2 * HALF :]])
    to_before = corr1[HALF:]
    early = jnp.concatenate(
        [corr0, corr1[: 2 * HALF], shifted(to_after, 1), shifted(to_before, -1)]
    )
    late = jnp.concatenate([shifted(corr2, 1), shifted(corr2, -1)])

    slot_ids = jnp.arange(slots, dtype=jnp.int32)

    def targets(source, round_index, owner):
        index = pair_local if owner == 0 else pair_partner
        live = slot_ids < pair_count[source, round_index]
        hit = live & (pair_owner[source, round_index] == owner)
        row = index[source, round_index] * BINS + pair_bin[source, round_index]
        return jnp.where(hit, row, -1)

    live0 = slot_ids < pair_count[block, 0]
    chan0 = jnp.where(pair_owner[block, 0] == 0, pair_local[block, 0], pair_partner[block, 0])
    row0 = jnp.where(live0, chan0 * BINS + pair_bin[block, 0], -1)
    near0, near1 = targets(block, 1, 0), targets(before, 1, 1)
    far0, far1 = targets(block, 2, 0), targets(before2, 2, 1)
    ids = jnp.concatenate(
        [
            row0,
            near0[:HALF],
            near1[HALF:],
            near1[:HALF],
            far1[:HALF],
            near0[HALF:],
            far0[:HALF],
            far1[HALF:],
            far0[HALF:],
        ]
    )[None, :]
    place = core ^ flip
    return final(
        place, ids, early, swapped(early, "seg", 1), late, swapped(late, "seg", 1), chans
    )


def solution(mesh):
    return jax.shard_map(
        per_device,
        mesh=mesh,
        in_specs=(P("seg", "chan", None, "lag"), P(), P(), P(), P(), P()),
        out_specs=P("chan", None, "lag"),
        check_vma=False,
    )
```

```python
import functools
import math

import jax
import jax.numpy as jnp
from jax import lax
from jax.experimental import pallas as pl
from jax.experimental.pallas import tpu as pltpu
from jax.sharding import PartitionSpec as P

FREQ = 6144
LAGS = 2048
BINS = 2
HALF = 128
QUARTER = LAGS // 4
TILE = 512
PICK_MB = 20
CORR_MB = 56
SPLIT = 128
F32 = jnp.float32
BF16 = jnp.bfloat16


def route(axis, move):
    return [(i, move(i)) for i in range(lax.axis_size(axis))]


def shifted(value, distance):
    count = lax.axis_size("chan")
    return lax.ppermute(value, "chan", route("chan", lambda i: (i + distance) % count))


def swapped(value, axis, bit):
    return lax.ppermute(value, axis, route(axis, lambda i: i ^ bit))


def params(megabytes=32):
    return pltpu.CompilerParams(vmem_limit_bytes=megabytes << 20)


def dot(a, b):
    return jnp.dot(a, b, preferred_element_type=F32)


def cost(flops, moved):
    return pl.CostEstimate(flops=flops, bytes_accessed=moved, transcendentals=0)


def pick_kernel(index_ref, rows_ref, *refs):
    outs, hot_ref = refs[:-1], refs[-1]

    @pl.when(pl.program_id(0) == 0)
    def _():
        ids = lax.broadcasted_iota(jnp.int32, hot_ref.shape, 1)
        hot_ref[...] = jnp.where(index_ref[...] == ids, 1.0, 0.0).astype(BF16)

    for part in range(2):
        picked = dot(hot_ref[...], rows_ref[part]).astype(BF16)
        row = 0
        for out_ref in outs:
            count = out_ref.shape[1]
            out_ref[part] = picked[row : row + count]
            row += count


def pick(groups, rows, megabytes=PICK_MB):
    counts = [sum(index.shape[0] for index in group) for group in groups]
    index = jnp.concatenate([index for group in groups for index in group])
    (total,), (_, chans, freqs) = index.shape, rows.shape
    return pl.pallas_call(
        pick_kernel,
        out_shape=[jax.ShapeDtypeStruct((2, count, freqs), BF16) for count in counts],
        grid=(freqs // TILE,),
        in_specs=[
            pl.BlockSpec((total, 1), lambda i: (0, 0)),
            pl.BlockSpec((2, chans, TILE), lambda i: (0, 0, i)),
        ],
        out_specs=[pl.BlockSpec((2, count, TILE), lambda i: (0, 0, i)) for count in counts],
        scratch_shapes=[pltpu.VMEM((total, chans), BF16)],
        compiler_params=params(megabytes),
        cost_estimate=cost(4 * total * chans * freqs, 4 * (chans + total) * freqs),
        name="pick",
    )(index[:, None], rows)


def table_kernel(cos_a_ref, sin_a_ref, cos_b_ref, sin_b_ref, sign_ref, cos_ref, sin_ref):
    cos_b, sin_b = cos_b_ref[...], sin_b_ref[...]
    width = cos_b.shape[1]
    for step in range(2 * QUARTER // width):
        cos_a, sin_a = cos_a_ref[:, step : step + 1], sin_a_ref[:, step : step + 1]
        cols = slice(step * width, (step + 1) * width)
        cos_ref[:, cols] = (cos_a * cos_b - sin_a * sin_b).astype(BF16)
        sin_ref[:, cols] = (sign_ref[0] * (sin_a * cos_b + cos_a * sin_b)).astype(BF16)


def waves(doubled, freq):
    angle = jnp.mod(doubled * freq, 4 * FREQ).astype(F32) * (math.pi / (2 * FREQ))
    return jnp.cos(angle), jnp.sin(angle)


def lag_waves(freq_index, core):
    width = 128
    steps = 2 * QUARTER // width
    flat = jnp.arange(freq_index.shape[0] * steps, dtype=jnp.int32)
    step = flat % steps
    start = (core ^ (step // (steps // 2))) * QUARTER + (step % (steps // 2)) * width
    coarse = lax.optimization_barrier(waves(2 * start, freq_index[0] + flat // steps))
    cos_a, sin_a = [value.reshape(-1, steps) for value in coarse]
    odd = 2 * jnp.arange(width, dtype=jnp.int32) + 1
    cos_a, sin_a = lax.optimization_barrier((cos_a, sin_a))
    return (cos_a, sin_a) + waves(odd[None, :], freq_index[:, None])


def lag_table(four, sign):
    freqs = four[0].shape[0]
    return pl.pallas_call(
        table_kernel,
        out_shape=[jax.ShapeDtypeStruct((freqs, 2 * QUARTER), BF16)] * 2,
        grid=(freqs // TILE,),
        in_specs=[pl.BlockSpec((TILE, v.shape[1]), lambda i: (i, 0)) for v in four]
        + [pl.BlockSpec(memory_space=pltpu.SMEM)],
        out_specs=[pl.BlockSpec((TILE, 2 * QUARTER), lambda i: (i, 0))] * 2,
        compiler_params=params(CORR_MB),
        cost_estimate=cost(12 * freqs * LAGS, 4 * freqs * LAGS),
        name="table",
    )(*four, sign[None])


def corr_kernel(count, *refs):
    firsts, seconds = refs[:count], refs[count : 2 * count]
    turn_ref, cos_ref, sin_ref, keep_ref, send_ref, cos_acc, sin_acc = refs[2 * count :]
    step = pl.program_id(0)

    @pl.when(step == 0)
    def _():
        cos_acc[...] = jnp.zeros_like(cos_acc)
        sin_acc[...] = jnp.zeros_like(sin_acc)

    turn_cos, turn_sin = turn_ref[0:1], turn_ref[1:2]
    row = 0
    for first_ref, second_ref in zip(firsts, seconds):
        first_re, first_im = first_ref[0].astype(F32), first_ref[1].astype(F32)
        second_re, second_im = second_ref[0].astype(F32), second_ref[1].astype(F32)
        real = first_re * second_re + first_im * second_im
        imag = first_im * second_re - first_re * second_im
        turned_re = (real * turn_cos + imag * turn_sin).astype(BF16)
        turned_im = (imag * turn_cos - real * turn_sin).astype(BF16)
        here = slice(row, row + first_ref.shape[1])
        cos_acc[here] += dot(turned_re, cos_ref[...])
        sin_acc[here] += dot(turned_im, sin_ref[...])
        row += first_ref.shape[1]

    @pl.when(step == pl.num_programs(0) - 1)
    def _():
        scale = FREQ ** (-0.5)
        total = (cos_acc[...] + sin_acc[...]) * scale
        other = (cos_acc[...] - sin_acc[...]) * scale
        keep_ref[0] = total[:, :QUARTER]
        keep_ref[1] = other[:, :QUARTER]
        send_ref[0] = total[:, QUARTER:].astype(BF16)
        send_ref[1] = other[:, QUARTER:].astype(BF16)


def correlate(pairs, turn, table):
    firsts, seconds = zip(*pairs)
    rows = sum(count for _, count, _ in firsts)
    freqs = table[0].shape[0]

    def spec(value):
        _, count, place = value
        return pl.BlockSpec((2, count, TILE), lambda i: (0, place, i))

    flat = firsts + seconds
    return pl.pallas_call(
        functools.partial(corr_kernel, len(pairs)),
        out_shape=(
            jax.ShapeDtypeStruct((2, rows, QUARTER), F32),
            jax.ShapeDtypeStruct((2, rows, QUARTER), BF16),
        ),
        grid=(freqs // TILE,),
        in_specs=[spec(value) for value in flat]
        + [
            pl.BlockSpec((2, TILE), lambda i: (0, i)),
            pl.BlockSpec((TILE, 2 * QUARTER), lambda i: (i, 0)),
            pl.BlockSpec((TILE, 2 * QUARTER), lambda i: (i, 0)),
        ],
        out_specs=(
            pl.BlockSpec((2, rows, QUARTER), lambda i: (0, 0, 0)),
            pl.BlockSpec((2, rows, QUARTER), lambda i: (0, 0, 0)),
        ),
        scratch_shapes=[pltpu.VMEM((rows, 2 * QUARTER), F32)] * 2,
        compiler_params=params(CORR_MB),
        cost_estimate=cost(4 * rows * freqs * LAGS, 4 * freqs * LAGS + 16 * rows * freqs),
        name="corr",
    )(*[value[0] for value in flat], turn, *table)


def fold_kernel(keep_ref, other_ref, mine_ref, far_ref):
    mine_ref[...] = (keep_ref[0] + other_ref[0].astype(F32)).astype(BF16)
    far_ref[...] = (keep_ref[1] + other_ref[1].astype(F32)).astype(BF16)


def fold(keep, other):
    shape = jax.ShapeDtypeStruct(keep.shape[1:], BF16)
    return pl.pallas_call(
        fold_kernel, out_shape=(shape, shape), compiler_params=params(), name="fold"
    )(keep, other)


def add_kernel(mine_ref, near_ref, out_ref):
    out_ref[...] = (mine_ref[...].astype(F32) + near_ref[...].astype(F32)).astype(BF16)


def sum_kernel(flip_ref, *refs):
    parts, out_ref = refs[:-1], refs[-1]
    sums = [
        a[...].astype(F32) + b[...].astype(F32) for a, b in zip(parts[::2], parts[1::2])
    ]
    total = functools.reduce(lambda a, b: a + b, sums).astype(BF16)
    size = total.shape[1]
    row = lax.broadcasted_iota(jnp.int32, (size, size), 0)
    col = lax.broadcasted_iota(jnp.int32, (size, size), 1)
    wanted = jnp.where(flip_ref[0] == 1, size - 1 - col, col)
    order = jnp.where(row == wanted, 1.0, 0.0).astype(BF16)
    out_ref[...] = dot(total, order).astype(BF16)


def summed(flip, parts):
    vmem = pl.BlockSpec(memory_space=pltpu.VMEM)
    return pl.pallas_call(
        sum_kernel,
        out_shape=jax.ShapeDtypeStruct(parts[0].shape, BF16),
        in_specs=[pl.BlockSpec(memory_space=pltpu.SMEM)] + [vmem] * len(parts),
        compiler_params=params(),
        name="sum",
    )(flip[None], *parts)


def folded(partial):
    keep, send = partial
    return fold(keep, swapped(send, "seg", 1))


def near_sum(mine, far):
    return pl.pallas_call(
        add_kernel,
        out_shape=jax.ShapeDtypeStruct(mine.shape, BF16),
        compiler_params=params(),
        name="add",
    )(mine, swapped(far, "lag", 1))


def far_sum(both, flip):
    return summed(flip, [both, swapped(both, "seg", 2)])


def direct_sum(mine, far, flip):
    near = swapped(far, "lag", 1)
    opposite = swapped(mine, "seg", 2)
    seg, lag = lax.axis_size("seg"), lax.axis_size("lag")
    pairs = [(s * lag + g, (s ^ 2) * lag + (g ^ 1)) for s in range(seg) for g in range(lag)]
    across = lax.ppermute(far, ("seg", "lag"), pairs)
    return summed(flip, [mine, near, opposite, across])


def final_kernel(at_ref, ids_ref, early_ref, early2_ref, late_ref, late2_ref, out_ref):
    chans = out_ref.shape[0]
    base = pl.program_id(0) * chans
    early = early_ref.shape[0]
    slots = ids_ref.shape[1]
    for bin_index in range(BINS):
        chan = base + lax.broadcasted_iota(jnp.int32, (chans, slots), 0)
        hot = jnp.where(ids_ref[...] == chan * BINS + bin_index, 1.0, 0.0).astype(BF16)
        mine = dot(hot[:, :early], early_ref[...]) + dot(hot[:, early:], late_ref[...])
        other = dot(hot[:, :early], early2_ref[...]) + dot(hot[:, early:], late2_ref[...])
        low = at_ref[0] == 0
        out_ref[:, bin_index, :QUARTER] = jnp.where(low, mine, other)
        out_ref[:, bin_index, QUARTER:] = jnp.where(low, other, mine)


def final(at, ids, early, early2, late, late2, chans):
    tile = 128
    whole = [pl.BlockSpec(v.shape, lambda i: (0, 0)) for v in (ids, early, early2, late, late2)]
    return pl.pallas_call(
        final_kernel,
        out_shape=jax.ShapeDtypeStruct((chans, BINS, LAGS // 2), F32),
        grid=(pl.cdiv(chans, tile),),
        in_specs=[pl.BlockSpec(memory_space=pltpu.SMEM)] + whole,
        out_specs=pl.BlockSpec((tile, BINS, LAGS // 2), lambda i: (i, 0, 0)),
        compiler_params=params(48),
        name="final",
    )(at[None], ids, early, early2, late, late2)


def per_device(spectra, pair_local, pair_partner, pair_bin, pair_owner, pair_count):
    block = lax.axis_index("chan")
    blocks = lax.axis_size("chan")
    lag_index = lax.axis_index("lag")
    core = lax.axis_index("seg") % 2
    own = spectra[0]
    chans, _, half_freq = own.shape
    slots = pair_local.shape[2]
    rows = own.transpose(1, 0, 2)
    before, before2 = (block - 1) % blocks, (block - 2) % blocks

    first_up = [pair_local[block, 1, HALF:], pair_local[block, 2, :SPLIT]]
    first_down = [pair_partner[before, 1, :HALF], pair_partner[before2, 2, :SPLIT]]
    last_up, last_down = pair_local[block, 2, SPLIT:], pair_partner[before2, 2, SPLIT:]
    picked = pick([first_up, first_down], rows)
    picked, rows, zero = lax.optimization_barrier((picked, rows, jnp.int32(0)))
    from_before, from_after = [shifted(picked[0], 1)], [shifted(picked[1], -1)]

    freq_index = lag_index * half_freq + jnp.arange(half_freq, dtype=jnp.int32) + 1 + zero
    four = lag_waves(freq_index, core)
    four, last_up, last_down = lax.optimization_barrier((four, last_up, last_down))
    local = [
        pair_local[block, 0],
        pair_partner[block, 0],
        pair_local[block, 1, :HALF],
        pair_partner[before, 1, HALF:],
    ]
    up, down, local = pick([[last_up], [last_down], local], rows, CORR_MB)
    up, down, local, four = lax.optimization_barrier((up, down, local, four))
    from_before.append(shifted(up, 1))
    from_after.append(shifted(down, -1))
    sign = jnp.where(lag_index == 0, 1.0, -1.0).astype(F32)
    table = lag_table(four, sign)
    angle = freq_index.astype(F32) * (math.pi / (2 * FREQ))
    turn = jnp.stack([jnp.cos(angle), jnp.sin(angle)])

    flip = 1 - lag_index

    def at(value, count, place):
        return value, count, place

    half0 = folded(correlate([(at(local, slots, 0), at(local, slots, 1))], turn, table))
    both0, above, below = lax.optimization_barrier(
        (near_sum(*half0), from_before[0], from_after[0])
    )
    pairs = [
        (at(local, HALF, 4), at(below, HALF, 0)),
        (at(above, HALF, 0), at(local, HALF, 5)),
        (at(above, SPLIT, HALF // SPLIT), at(below, SPLIT, HALF // SPLIT)),
    ]
    half1 = folded(correlate(pairs, turn, table))
    corr0 = far_sum(both0, flip)
    both1, above, below = lax.optimization_barrier(
        (near_sum(*half1), from_before[1], from_after[1])
    )
    corr1 = far_sum(both1, flip)
    tail = slots - SPLIT
    half2 = folded(correlate([(at(above, tail, 0), at(below, tail, 0))], turn, table))
    corr2 = direct_sum(*half2, flip)
    to_after = jnp.concatenate([corr1[:HALF], corr1[2 * HALF :]])
    to_before = corr1[HALF:]
    early = jnp.concatenate(
        [corr0, corr1[: 2 * HALF], shifted(to_after, 1), shifted(to_before, -1)]
    )
    late = jnp.concatenate([shifted(corr2, 1), shifted(corr2, -1)])

    slot_ids = jnp.arange(slots, dtype=jnp.int32)

    def targets(source, round_index, owner):
        index = pair_local if owner == 0 else pair_partner
        live = slot_ids < pair_count[source, round_index]
        hit = live & (pair_owner[source, round_index] == owner)
        row = index[source, round_index] * BINS + pair_bin[source, round_index]
        return jnp.where(hit, row, -1)

    live0 = slot_ids < pair_count[block, 0]
    chan0 = jnp.where(pair_owner[block, 0] == 0, pair_local[block, 0], pair_partner[block, 0])
    row0 = jnp.where(live0, chan0 * BINS + pair_bin[block, 0], -1)
    near0, near1 = targets(block, 1, 0), targets(before, 1, 1)
    far0, far1 = targets(block, 2, 0), targets(before2, 2, 1)
    ids = jnp.concatenate(
        [
            row0,
            near0[:HALF],
            near1[HALF:],
            near1[:HALF],
            far1[:SPLIT],
            near0[HALF:],
            far0[:SPLIT],
            far1[SPLIT:],
            far0[SPLIT:],
        ]
    )[None, :]
    place = core ^ flip
    return final(
        place, ids, early, swapped(early, "seg", 1), late, swapped(late, "seg", 1), chans
    )


def solution(mesh):
    return jax.shard_map(
        per_device,
        mesh=mesh,
        in_specs=(P("seg", "chan", None, "lag"), P(), P(), P(), P(), P()),
        out_specs=P("chan", None, "lag"),
        check_vma=False,
    )
```

```python
import functools
import math

import jax
import jax.numpy as jnp
from jax import lax
from jax.experimental import pallas as pl
from jax.experimental.pallas import tpu as pltpu
from jax.sharding import PartitionSpec as P

FREQ = 6144
LAGS = 2048
BINS = 2
HALF = 128
QUARTER = LAGS // 4
TILE = 512
PICK_MB = 20
CORR_MB = 56
SPLIT = 128
F32 = jnp.float32
BF16 = jnp.bfloat16


def route(axis, move):
    return [(i, move(i)) for i in range(lax.axis_size(axis))]


def shifted(value, distance):
    count = lax.axis_size("chan")
    return lax.ppermute(value, "chan", route("chan", lambda i: (i + distance) % count))


def swapped(value, axis, bit):
    return lax.ppermute(value, axis, route(axis, lambda i: i ^ bit))


def params(megabytes=32):
    return pltpu.CompilerParams(vmem_limit_bytes=megabytes << 20)


def dot(a, b):
    return jnp.dot(a, b, preferred_element_type=F32)


def cost(flops, moved):
    return pl.CostEstimate(flops=flops, bytes_accessed=moved, transcendentals=0)


def pick_kernel(index_ref, rows_ref, *refs):
    outs, hot_ref = refs[:-1], refs[-1]

    @pl.when(pl.program_id(0) == 0)
    def _():
        ids = lax.broadcasted_iota(jnp.int32, hot_ref.shape, 1)
        hot_ref[...] = jnp.where(index_ref[...] == ids, 1.0, 0.0).astype(BF16)

    for part in range(2):
        picked = dot(hot_ref[...], rows_ref[part]).astype(BF16)
        row = 0
        for out_ref in outs:
            count = out_ref.shape[1]
            out_ref[part] = picked[row : row + count]
            row += count


def pick(groups, rows, megabytes=PICK_MB):
    counts = [sum(index.shape[0] for index in group) for group in groups]
    index = jnp.concatenate([index for group in groups for index in group])
    (total,), (_, chans, freqs) = index.shape, rows.shape
    return pl.pallas_call(
        pick_kernel,
        out_shape=[jax.ShapeDtypeStruct((2, count, freqs), BF16) for count in counts],
        grid=(freqs // TILE,),
        in_specs=[
            pl.BlockSpec((total, 1), lambda i: (0, 0)),
            pl.BlockSpec((2, chans, TILE), lambda i: (0, 0, i)),
        ],
        out_specs=[pl.BlockSpec((2, count, TILE), lambda i: (0, 0, i)) for count in counts],
        scratch_shapes=[pltpu.VMEM((total, chans), BF16)],
        compiler_params=params(megabytes),
        cost_estimate=cost(4 * total * chans * freqs, 4 * (chans + total) * freqs),
        name="pick",
    )(index[:, None], rows)


def table_kernel(cos_a_ref, sin_a_ref, cos_b_ref, sin_b_ref, sign_ref, cos_ref, sin_ref):
    cos_b, sin_b = cos_b_ref[...], sin_b_ref[...]
    width = cos_b.shape[1]
    for step in range(2 * QUARTER // width):
        cos_a, sin_a = cos_a_ref[:, step : step + 1], sin_a_ref[:, step : step + 1]
        cols = slice(step * width, (step + 1) * width)
        cos_ref[:, cols] = (cos_a * cos_b - sin_a * sin_b).astype(BF16)
        sin_ref[:, cols] = (sign_ref[0] * (sin_a * cos_b + cos_a * sin_b)).astype(BF16)


def waves(doubled, freq):
    angle = jnp.mod(doubled * freq, 4 * FREQ).astype(F32) * (math.pi / (2 * FREQ))
    return jnp.cos(angle), jnp.sin(angle)


def lag_waves(freq_index, core):
    width = 128
    steps = 2 * QUARTER // width
    flat = jnp.arange(freq_index.shape[0] * steps, dtype=jnp.int32)
    step = flat % steps
    start = (core ^ (step // (steps // 2))) * QUARTER + (step % (steps // 2)) * width
    coarse = lax.optimization_barrier(waves(2 * start, freq_index[0] + flat // steps))
    cos_a, sin_a = [value.reshape(-1, steps) for value in coarse]
    odd = 2 * jnp.arange(width, dtype=jnp.int32) + 1
    cos_a, sin_a = lax.optimization_barrier((cos_a, sin_a))
    return (cos_a, sin_a) + waves(odd[None, :], freq_index[:, None])


def lag_table(four, sign):
    freqs = four[0].shape[0]
    return pl.pallas_call(
        table_kernel,
        out_shape=[jax.ShapeDtypeStruct((freqs, 2 * QUARTER), BF16)] * 2,
        grid=(freqs // TILE,),
        in_specs=[pl.BlockSpec((TILE, v.shape[1]), lambda i: (i, 0)) for v in four]
        + [pl.BlockSpec(memory_space=pltpu.SMEM)],
        out_specs=[pl.BlockSpec((TILE, 2 * QUARTER), lambda i: (i, 0))] * 2,
        compiler_params=params(CORR_MB),
        cost_estimate=cost(12 * freqs * LAGS, 4 * freqs * LAGS),
        name="table",
    )(*four, sign[None])


def corr_kernel(count, *refs):
    firsts, seconds = refs[:count], refs[count : 2 * count]
    turn_ref, cos_ref, sin_ref, keep_ref, send_ref, cos_acc, sin_acc = refs[2 * count :]
    step = pl.program_id(0)

    @pl.when(step == 0)
    def _():
        cos_acc[...] = jnp.zeros_like(cos_acc)
        sin_acc[...] = jnp.zeros_like(sin_acc)

    turn_cos, turn_sin = turn_ref[0:1], turn_ref[1:2]
    row = 0
    for first_ref, second_ref in zip(firsts, seconds):
        first_re, first_im = first_ref[0].astype(F32), first_ref[1].astype(F32)
        second_re, second_im = second_ref[0].astype(F32), second_ref[1].astype(F32)
        real = first_re * second_re + first_im * second_im
        imag = first_im * second_re - first_re * second_im
        turned_re = (real * turn_cos + imag * turn_sin).astype(BF16)
        turned_im = (imag * turn_cos - real * turn_sin).astype(BF16)
        here = slice(row, row + first_ref.shape[1])
        cos_acc[here] += dot(turned_re, cos_ref[...])
        sin_acc[here] += dot(turned_im, sin_ref[...])
        row += first_ref.shape[1]

    @pl.when(step == pl.num_programs(0) - 1)
    def _():
        scale = FREQ ** (-0.5)
        total = (cos_acc[...] + sin_acc[...]) * scale
        other = (cos_acc[...] - sin_acc[...]) * scale
        keep_ref[0] = total[:, :QUARTER]
        keep_ref[1] = other[:, :QUARTER]
        send_ref[0] = total[:, QUARTER:].astype(BF16)
        send_ref[1] = other[:, QUARTER:].astype(BF16)


def correlate(pairs, turn, table):
    firsts, seconds = zip(*pairs)
    rows = sum(count for _, count, _ in firsts)
    freqs = table[0].shape[0]

    def spec(value):
        _, count, place = value
        return pl.BlockSpec((2, count, TILE), lambda i: (0, place, i))

    flat = firsts + seconds
    return pl.pallas_call(
        functools.partial(corr_kernel, len(pairs)),
        out_shape=(
            jax.ShapeDtypeStruct((2, rows, QUARTER), F32),
            jax.ShapeDtypeStruct((2, rows, QUARTER), BF16),
        ),
        grid=(freqs // TILE,),
        in_specs=[spec(value) for value in flat]
        + [
            pl.BlockSpec((2, TILE), lambda i: (0, i)),
            pl.BlockSpec((TILE, 2 * QUARTER), lambda i: (i, 0)),
            pl.BlockSpec((TILE, 2 * QUARTER), lambda i: (i, 0)),
        ],
        out_specs=(
            pl.BlockSpec((2, rows, QUARTER), lambda i: (0, 0, 0)),
            pl.BlockSpec((2, rows, QUARTER), lambda i: (0, 0, 0)),
        ),
        scratch_shapes=[pltpu.VMEM((rows, 2 * QUARTER), F32)] * 2,
        compiler_params=params(CORR_MB),
        cost_estimate=cost(4 * rows * freqs * LAGS, 4 * freqs * LAGS + 16 * rows * freqs),
        name="corr",
    )(*[value[0] for value in flat], turn, *table)


def fold_kernel(keep_ref, other_ref, mine_ref, far_ref):
    mine_ref[...] = (keep_ref[0] + other_ref[0].astype(F32)).astype(mine_ref.dtype)
    far_ref[...] = (keep_ref[1] + other_ref[1].astype(F32)).astype(BF16)


def fold(keep, other, mine_type):
    shapes = [jax.ShapeDtypeStruct(keep.shape[1:], kind) for kind in (mine_type, BF16)]
    return pl.pallas_call(
        fold_kernel, out_shape=shapes, compiler_params=params(), name="fold"
    )(keep, other)


def add_kernel(mine_ref, near_ref, out_ref):
    out_ref[...] = (mine_ref[...].astype(F32) + near_ref[...].astype(F32)).astype(BF16)


def sum_kernel(flip_ref, *refs):
    parts, out_ref = refs[:-1], refs[-1]
    sums = [
        a[...].astype(F32) + b[...].astype(F32) for a, b in zip(parts[::2], parts[1::2])
    ]
    total = functools.reduce(lambda a, b: a + b, sums).astype(BF16)
    size = total.shape[1]
    row = lax.broadcasted_iota(jnp.int32, (size, size), 0)
    col = lax.broadcasted_iota(jnp.int32, (size, size), 1)
    wanted = jnp.where(flip_ref[0] == 1, size - 1 - col, col)
    order = jnp.where(row == wanted, 1.0, 0.0).astype(BF16)
    out_ref[...] = dot(total, order).astype(BF16)


def summed(flip, parts):
    vmem = pl.BlockSpec(memory_space=pltpu.VMEM)
    return pl.pallas_call(
        sum_kernel,
        out_shape=jax.ShapeDtypeStruct(parts[0].shape, BF16),
        in_specs=[pl.BlockSpec(memory_space=pltpu.SMEM)] + [vmem] * len(parts),
        compiler_params=params(),
        name="sum",
    )(flip[None], *parts)


def folded(partial, mine_type=F32):
    keep, send = partial
    return fold(keep, swapped(send, "seg", 1), mine_type)


def near_sum(mine, far):
    return pl.pallas_call(
        add_kernel,
        out_shape=jax.ShapeDtypeStruct(mine.shape, BF16),
        compiler_params=params(),
        name="add",
    )(mine, swapped(far, "lag", 1))


def far_sum(both, flip):
    return summed(flip, [both, swapped(both, "seg", 2)])


def direct_sum(mine, far, flip):
    near = swapped(far, "lag", 1)
    opposite = swapped(mine, "seg", 2)
    seg, lag = lax.axis_size("seg"), lax.axis_size("lag")
    pairs = [(s * lag + g, (s ^ 2) * lag + (g ^ 1)) for s in range(seg) for g in range(lag)]
    across = lax.ppermute(far, ("seg", "lag"), pairs)
    return summed(flip, [mine, near, opposite, across])


def final_kernel(at_ref, ids_ref, early_ref, early2_ref, late_ref, late2_ref, out_ref):
    chans = out_ref.shape[0]
    base = pl.program_id(0) * chans
    early = early_ref.shape[0]
    slots = ids_ref.shape[1]
    for bin_index in range(BINS):
        chan = base + lax.broadcasted_iota(jnp.int32, (chans, slots), 0)
        hot = jnp.where(ids_ref[...] == chan * BINS + bin_index, 1.0, 0.0).astype(BF16)
        mine = dot(hot[:, :early], early_ref[...]) + dot(hot[:, early:], late_ref[...])
        other = dot(hot[:, :early], early2_ref[...]) + dot(hot[:, early:], late2_ref[...])
        low = at_ref[0] == 0
        out_ref[:, bin_index, :QUARTER] = jnp.where(low, mine, other)
        out_ref[:, bin_index, QUARTER:] = jnp.where(low, other, mine)


def final(at, ids, early, early2, late, late2, chans):
    tile = 128
    whole = [pl.BlockSpec(v.shape, lambda i: (0, 0)) for v in (ids, early, early2, late, late2)]
    return pl.pallas_call(
        final_kernel,
        out_shape=jax.ShapeDtypeStruct((chans, BINS, LAGS // 2), F32),
        grid=(pl.cdiv(chans, tile),),
        in_specs=[pl.BlockSpec(memory_space=pltpu.SMEM)] + whole,
        out_specs=pl.BlockSpec((tile, BINS, LAGS // 2), lambda i: (i, 0, 0)),
        compiler_params=params(48),
        name="final",
    )(at[None], ids, early, early2, late, late2)


def per_device(spectra, pair_local, pair_partner, pair_bin, pair_owner, pair_count):
    block = lax.axis_index("chan")
    blocks = lax.axis_size("chan")
    lag_index = lax.axis_index("lag")
    core = lax.axis_index("seg") % 2
    own = spectra[0]
    chans, _, half_freq = own.shape
    slots = pair_local.shape[2]
    rows = own.transpose(1, 0, 2)
    before, before2 = (block - 1) % blocks, (block - 2) % blocks

    first_up = [pair_local[block, 1, HALF:], pair_local[block, 2, :SPLIT]]
    first_down = [pair_partner[before, 1, :HALF], pair_partner[before2, 2, :SPLIT]]
    last_up, last_down = pair_local[block, 2, SPLIT:], pair_partner[before2, 2, SPLIT:]
    picked = pick([first_up, first_down], rows)
    picked, rows, zero = lax.optimization_barrier((picked, rows, jnp.int32(0)))
    from_before, from_after = [shifted(picked[0], 1)], [shifted(picked[1], -1)]

    freq_index = lag_index * half_freq + jnp.arange(half_freq, dtype=jnp.int32) + 1 + zero
    four = lag_waves(freq_index, core)
    four, last_up, last_down = lax.optimization_barrier((four, last_up, last_down))
    local = [
        pair_local[block, 0],
        pair_partner[block, 0],
        pair_local[block, 1, :HALF],
        pair_partner[before, 1, HALF:],
    ]
    up, down, local = pick([[last_up], [last_down], local], rows, CORR_MB)
    up, down, local, four = lax.optimization_barrier((up, down, local, four))
    from_before.append(shifted(up, 1))
    from_after.append(shifted(down, -1))
    sign = jnp.where(lag_index == 0, 1.0, -1.0).astype(F32)
    table = lag_table(four, sign)
    angle = freq_index.astype(F32) * (math.pi / (2 * FREQ))
    turn = jnp.stack([jnp.cos(angle), jnp.sin(angle)])

    flip = 1 - lag_index

    def at(value, count, place):
        return value, count, place

    half0 = folded(correlate([(at(local, slots, 0), at(local, slots, 1))], turn, table))
    both0, above, below = lax.optimization_barrier(
        (near_sum(*half0), from_before[0], from_after[0])
    )
    pairs = [
        (at(local, HALF, 4), at(below, HALF, 0)),
        (at(above, HALF, 0), at(local, HALF, 5)),
        (at(above, SPLIT, HALF // SPLIT), at(below, SPLIT, HALF // SPLIT)),
    ]
    half1 = folded(correlate(pairs, turn, table))
    corr0 = far_sum(both0, flip)
    both1, above, below = lax.optimization_barrier(
        (near_sum(*half1), from_before[1], from_after[1])
    )
    corr1 = far_sum(both1, flip)
    tail = slots - SPLIT
    half2 = folded(correlate([(at(above, tail, 0), at(below, tail, 0))], turn, table), BF16)
    corr2 = direct_sum(*half2, flip)
    to_after = jnp.concatenate([corr1[:HALF], corr1[2 * HALF :]])
    to_before = corr1[HALF:]
    early = jnp.concatenate(
        [corr0, corr1[: 2 * HALF], shifted(to_after, 1), shifted(to_before, -1)]
    )
    late = jnp.concatenate([shifted(corr2, 1), shifted(corr2, -1)])

    slot_ids = jnp.arange(slots, dtype=jnp.int32)

    def targets(source, round_index, owner):
        index = pair_local if owner == 0 else pair_partner
        live = slot_ids < pair_count[source, round_index]
        hit = live & (pair_owner[source, round_index] == owner)
        row = index[source, round_index] * BINS + pair_bin[source, round_index]
        return jnp.where(hit, row, -1)

    live0 = slot_ids < pair_count[block, 0]
    chan0 = jnp.where(pair_owner[block, 0] == 0, pair_local[block, 0], pair_partner[block, 0])
    row0 = jnp.where(live0, chan0 * BINS + pair_bin[block, 0], -1)
    near0, near1 = targets(block, 1, 0), targets(before, 1, 1)
    far0, far1 = targets(block, 2, 0), targets(before2, 2, 1)
    ids = jnp.concatenate(
        [
            row0,
            near0[:HALF],
            near1[HALF:],
            near1[:HALF],
            far1[:SPLIT],
            near0[HALF:],
            far0[:SPLIT],
            far1[SPLIT:],
            far0[SPLIT:],
        ]
    )[None, :]
    place = core ^ flip
    return final(
        place, ids, early, swapped(early, "seg", 1), late, swapped(late, "seg", 1), chans
    )


def solution(mesh):
    return jax.shard_map(
        per_device,
        mesh=mesh,
        in_specs=(P("seg", "chan", None, "lag"), P(), P(), P(), P(), P()),
        out_specs=P("chan", None, "lag"),
        check_vma=False,
    )
```
